32 devices in a mesh: track: 2 (over y), tm: 16 (over z, x, core).
Axes of the slice: x: 2, y: 2, z: 4, core: 2. Of those that a mesh axis runs over, the one named last changes fastest.
Arguments:
- track_query: bfloat16 [16, 2048, 1024], P('track', 'tm'), may hold values from -6 to 6
- track_key: bfloat16 [16, 2048, 1024], P('track', 'tm'), may hold values from -6 to 6
- track_value: bfloat16 [16, 2048, 1024], P('track', 'tm'), may hold values from -6 to 6
- log_decay: float32 [16, 8, 2048], P('track', None, 'tm'), may hold values from -2.3 to 0
- valid_length: int32 [16], replicated, may hold values from 512 to 2048, as said below
- initial_state: bfloat16 [16, 8, 128, 128], P('track'), may hold values from -24 to 24
- cross_query: bfloat16 [16, 2048, 1024], P('track', 'tm'), may hold values from -5 to 5
- cross_key: bfloat16 [16, 2048, 1024], P('track', 'tm'), may hold values from -5 to 5
- grad_out: bfloat16 [16, 2048, 1024], P('track', 'tm'), may hold values from -6 to 6
Outputs:
- grad_query: bfloat16 [16, 2048, 1024], P('track', 'tm')
- grad_key: bfloat16 [16, 2048, 1024], P('track', 'tm')
- grad_value: bfloat16 [16, 2048, 1024], P('track', 'tm')
- grad_cross_query: bfloat16 [16, 2048, 1024], P('track', 'tm')
- grad_cross_key: bfloat16 [16, 2048, 1024], P('track', 'tm')
The draws below stay inside these ranges and needn't reach their ends.
Inputs may be any that keep to these rules, and one draw needn't show every extreme that they name: `valid_length`: multiples of 128; one track has 2048 valid steps and one has exactly 512.
All inputs are finite; a program needn't handle non-finite values.
Results may differ from the reference program's by a relative error of at most 0.005.
Values may be sent and summed in bfloat16 or wider, within the bound.
A program may use at most 256 MiB of HBM per device.

```python
import jax
import jax.numpy as jnp
from jax import lax

H = 8
DH = 128
D = 1024
VOICE_PARTS = 16
SEQUENCE_LENGTH = 2048
SHORT = 512


def draw_valid_length(key, part):
    first_key, second_key = jax.random.split(jax.random.fold_in(key, 11))
    blocks = jax.random.randint(first_key, (VOICE_PARTS,), SHORT // 128, SEQUENCE_LENGTH // 128 + 1)
    lengths = blocks * 128
    picked = jax.random.permutation(second_key, VOICE_PARTS)
    lengths = lengths.at[picked[0]].set(SEQUENCE_LENGTH)
    lengths = lengths.at[picked[1]].set(SHORT)
    return lengths.astype(jnp.int32)


def draw_log_decay(key, part):
    gathered_lookup_vectors = jax.random.split(jax.random.fold_in(key, 23), 6)
    share_fast = 0.35
    chooser = jax.random.uniform(gathered_lookup_vectors[0], (VOICE_PARTS, H))
    fast_rate = jnp.exp(jax.random.uniform(gathered_lookup_vectors[1], (VOICE_PARTS, H), minval=jnp.log(1.0 / 50.0), maxval=jnp.log(1.0 / 30.0)))
    slow_rate = jnp.exp(jax.random.uniform(gathered_lookup_vectors[2], (VOICE_PARTS, H), minval=jnp.log(0.05 / SEQUENCE_LENGTH), maxval=jnp.log(0.5 / SEQUENCE_LENGTH)))
    head_rate = jnp.where(chooser < share_fast, fast_rate, slow_rate)
    roughness = jnp.exp(jax.random.uniform(gathered_lookup_vectors[3], (VOICE_PARTS, H, SEQUENCE_LENGTH), minval=jnp.log(0.5), maxval=jnp.log(2.0)))
    forget_gate_logarithm = -head_rate[:, :, None] * roughness
    moment_indices = jax.random.randint(gathered_lookup_vectors[4], (VOICE_PARTS, 3), 0, SEQUENCE_LENGTH)
    segment_length = jax.random.uniform(gathered_lookup_vectors[5], (VOICE_PARTS, 3), minval=0.22, maxval=0.69)
    segment_count = jnp.zeros((VOICE_PARTS, SEQUENCE_LENGTH), jnp.float32)
    segment_count = segment_count.at[jnp.arange(VOICE_PARTS)[:, None], moment_indices].add(segment_length)
    return (forget_gate_logarithm - segment_count[:, None, :]).astype(jnp.float32)


def cross_pair(key):
    gathered_lookup_vectors = jax.random.split(jax.random.fold_in(key, 37), 2)
    full_shape = (VOICE_PARTS, SEQUENCE_LENGTH, D)
    query_draw = jnp.clip(jax.random.normal(gathered_lookup_vectors[0], full_shape), -5.0, 5.0)
    key_draw = jnp.clip(jax.random.normal(gathered_lookup_vectors[1], full_shape), -5.0, 5.0)
    return (query_draw, key_draw)


def draw_cross_query(key, part):
    return cross_pair(key)[0].astype(jnp.bfloat16)


def draw_cross_key(key, part):
    return cross_pair(key)[1].astype(jnp.bfloat16)


def block_levels(own_key, extent, pieces, low, high):
    gain = 1.0
    for dim, shards_of in pieces:
        heights = jax.random.uniform(jax.random.fold_in(jax.random.fold_in(own_key, 6), dim), (shards_of,), jnp.float32, low / len(pieces), high / len(pieces))
        gain = gain * jnp.repeat(jnp.exp(heights), extent[dim] // shards_of).reshape((-1,) + (1,) * (len(extent) - 1 - dim))
    return gain


def centred(own_key, extent, deviation, reach, cuts=(), kind=jnp.bfloat16):
    entries = deviation * jax.random.normal(own_key, extent, jnp.float32)
    if cuts:
        entries = entries * block_levels(own_key, extent, cuts, -0.22, 0.18)
    return jnp.clip(entries, -reach, reach).astype(kind)


def setup_inputs(seed: int = 0) -> dict:
    streams_of = jax.random.split(jax.random.key(seed), 10)
    track_query = centred(streams_of[0], (VOICE_PARTS, SEQUENCE_LENGTH, D), 1.0, 6.0, ((0, 2), (1, 16)))
    track_key = centred(streams_of[1], (VOICE_PARTS, SEQUENCE_LENGTH, D), 1.0, 6.0, ((0, 2), (1, 16)))
    track_value = centred(streams_of[2], (VOICE_PARTS, SEQUENCE_LENGTH, D), 1.0, 6.0, ((0, 2), (1, 16)))
    log_decay = draw_log_decay(jax.random.fold_in(streams_of[9], 71), 0)
    valid_length = draw_valid_length(jax.random.fold_in(streams_of[9], 71), 0)
    initial_state = centred(streams_of[5], (VOICE_PARTS, H, DH, DH), 4.0, 24.0, ((0, 2),))
    cross_query = draw_cross_query(jax.random.fold_in(streams_of[9], 71), 0)
    cross_key = draw_cross_key(jax.random.fold_in(streams_of[9], 71), 0)
    grad_out = centred(streams_of[8], (VOICE_PARTS, SEQUENCE_LENGTH, D), 1.0, 6.0, ((0, 2), (1, 16)))
    return {"track_query": track_query, "track_key": track_key, "track_value": track_value, "log_decay": log_decay, "valid_length": valid_length, "initial_state": initial_state, "cross_query": cross_query, "cross_key": cross_key, "grad_out": grad_out}


EPSILON = 1e-06
HIGHEST_PRECISION = lax.Precision.HIGHEST
BLOCK_ROWS = 128

def track_forward(query_rows, key_rows, value_rows, decay_rows, valid_rows, start_state):
    head_count = decay_rows.shape[0]
    total_rows = query_rows.shape[0]
    model_width = query_rows.shape[1]
    head_size = model_width // head_count
    blocks = total_rows // BLOCK_ROWS
    split_shape = (blocks, BLOCK_ROWS, head_count, head_size)
    query_float = query_rows.astype(jnp.float32).reshape(split_shape)
    key_float = (key_rows.astype(jnp.float32) * valid_rows[:, None]).reshape(split_shape)
    value_float = value_rows.astype(jnp.float32).reshape(split_shape)
    decay_split = jnp.transpose(decay_rows.reshape(head_count, blocks, BLOCK_ROWS), (1, 0, 2))
    lower_mask = jnp.arange(BLOCK_ROWS)[:, None] >= jnp.arange(BLOCK_ROWS)[None, :]

    def block_step(carry_state, inputs):
        query_block, key_block, value_block, decay_block = inputs
        within = jnp.cumsum(decay_block, axis=-1)
        decay_matrix = jnp.exp(jnp.where(lower_mask, within[:, :, None] - within[:, None, :], -jnp.inf))
        scores = jnp.einsum('thc,shc->hts', query_block, key_block, precision=HIGHEST_PRECISION) * decay_matrix
        from_start = jnp.transpose(jnp.exp(within))[:, :, None]
        to_end = jnp.transpose(jnp.exp(within[:, -1:] - within))[:, :, None]
        outputs = jnp.einsum('hts,shd->thd', scores, value_block, precision=HIGHEST_PRECISION)
        outputs = outputs + from_start * jnp.einsum('thc,hcd->thd', query_block, carry_state, precision=HIGHEST_PRECISION)
        new_state = jnp.exp(within[:, -1])[:, None, None] * carry_state
        new_state = new_state + jnp.einsum('shc,shd->hcd', key_block * to_end, value_block, precision=HIGHEST_PRECISION)
        return (new_state, outputs)
    initial = start_state.astype(jnp.float32)
    _, outputs = lax.scan(block_step, initial, (query_float, key_float, value_float, decay_split))
    outputs = outputs.reshape(total_rows, head_count, head_size)
    mean_square = lax.optimization_barrier(jnp.mean(outputs * outputs, axis=-1, keepdims=True))
    normed = outputs * (1.0 / jnp.sqrt(mean_square + EPSILON)) * valid_rows[:, None, None]
    return normed.astype(jnp.bfloat16).reshape(total_rows, model_width)

def cross_mix(cross_query, cross_key, normed, valid_mask):
    query_float = cross_query.astype(jnp.float32).reshape(VOICE_PARTS, SEQUENCE_LENGTH, H, DH)
    key_float = cross_key.astype(jnp.float32).reshape(VOICE_PARTS, SEQUENCE_LENGTH, H, DH)
    normed_float = normed.astype(jnp.float32).reshape(VOICE_PARTS, SEQUENCE_LENGTH, H, DH)
    logits = jnp.einsum('ithc,jthc->thij', query_float, key_float, precision=HIGHEST_PRECISION) / float(DH) ** 0.5
    logits = jnp.where(jnp.transpose(valid_mask)[:, None, None, :] > 0, logits, -1e+30)
    weights = jax.nn.softmax(logits, axis=-1)
    mixed = jnp.einsum('thij,jthd->ithd', weights, normed_float, precision=HIGHEST_PRECISION)
    return (mixed * valid_mask[:, :, None, None]).reshape(VOICE_PARTS, SEQUENCE_LENGTH, D)

def reference(track_query, track_key, track_value, log_decay, valid_length, initial_state, cross_query, cross_key, grad_out):
    time_index = jnp.arange(SEQUENCE_LENGTH)
    valid_mask = (time_index[None, :] < valid_length[:, None]).astype(jnp.float32)
    normed = lax.map(lambda packed: track_forward(packed[0], packed[1], packed[2], packed[3], packed[4], packed[5]), (track_query, track_key, track_value, log_decay, valid_mask, initial_state))

    def cross_only(query_in, key_in, normed_in):
        return cross_mix(query_in, key_in, normed_in, valid_mask)
    _, pullback = jax.vjp(cross_only, cross_query, cross_key, normed)
    grad_cross_query, grad_cross_key, grad_normed = pullback(grad_out.astype(jnp.float32))

    def track_backward(packed):

        def forward(query_in, key_in, value_in):
            return track_forward(query_in, key_in, value_in, packed[3], packed[4], packed[6])
        _, track_pull = jax.vjp(forward, packed[0], packed[1], packed[2])
        return track_pull(packed[5])
    grad_query, grad_key, grad_value = lax.map(track_backward, (track_query, track_key, track_value, log_decay, valid_mask, grad_normed, initial_state))
    return (grad_query, grad_key, grad_value, grad_cross_query, grad_cross_key)
```

```python
import functools

import jax
import jax.numpy as jnp
from jax import lax
from jax.experimental import pallas as pl
from jax.experimental.pallas import tpu as pltpu
from jax.sharding import PartitionSpec as P


EPSILON = 1e-06
MESH = pl.DeviceIdType.MESH
BF = jnp.bfloat16
F32 = jnp.float32
HEADS_PER_CHUNK = 2


def mm(a, b):
    return lax.dot_general(a, b, (((1,), (0,)), ((), ())), preferred_element_type=F32)


def mm_nt(a, b):
    return lax.dot_general(a, b, (((1,), (1,)), ((), ())), preferred_element_type=F32)


def mm_tn(a, b):
    return lax.dot_general(a, b, (((0,), (0,)), ((), ())), preferred_element_type=F32)


def entry_barrier(me, count):
    barrier = pltpu.get_barrier_semaphore()

    @pl.when(me > 0)
    def _():
        pl.semaphore_signal(barrier, inc=1, device_id={"tm": me - 1}, device_id_type=MESH)

    @pl.when(me < count - 1)
    def _():
        pl.semaphore_signal(barrier, inc=1, device_id={"tm": me + 1}, device_id_type=MESH)

    peers = jnp.where(me > 0, 1, 0) + jnp.where(me < count - 1, 1, 0)
    pl.semaphore_wait(barrier, peers)


def chunk_copy(send_buf, recv_buf, send_sem, recv_sem, chunk, per, target):
    return pltpu.make_async_remote_copy(
        src_ref=send_buf.at[pl.ds(chunk * per, per)],
        dst_ref=recv_buf.at[pl.ds(chunk * per, per)],
        send_sem=send_sem.at[chunk],
        recv_sem=recv_sem.at[chunk],
        device_id={"tm": target},
        device_id_type=MESH,
    )


def forward_kernel(
    count, heads, per, q_ref, k_ref, v_ref, col_ref, row_ref, init_ref,
    normed_ref, out_ref, state_ref, recv_buf, send_buf, send_sem, recv_sem,
):
    me = lax.axis_index("tm")
    tracks, rows, width = q_ref.shape
    size = width // heads
    chunks = heads // per
    total = tracks * chunks
    target = jnp.minimum(me + 1, count - 1)
    entry_barrier(me, count)

    @pl.when(me == 0)
    def _():
        def fill(i, carry):
            recv_buf[pl.ds(i * heads, heads)] = init_ref[pl.ds(i * heads, heads)].astype(F32)
            return carry

        lax.fori_loop(0, tracks, fill, 0)

    t_index = lax.broadcasted_iota(jnp.int32, (rows, rows), 0)
    s_index = lax.broadcasted_iota(jnp.int32, (rows, rows), 1)
    lower = t_index >= s_index

    def one_track(x, carry):
        cols = col_ref[x]
        valid = cols[:, heads : heads + 1]
        from_start = jnp.exp(cols)
        to_end = jnp.exp(cols[rows - 1 : rows, :] - cols)
        for part in range(chunks):
            chunk = x * chunks + part
            sums = []
            keys = []
            for lane in range(per):
                h = part * per + lane
                cut = slice(h * size, (h + 1) * size)
                k_float = k_ref[x, :, cut].astype(F32) * valid
                keys.append(k_float.astype(BF))
                sums.append(mm_tn((k_float * to_end[:, h : h + 1]).astype(BF), v_ref[x, :, cut]))

            @pl.when(me > 0)
            def _():
                chunk_copy(send_buf, recv_buf, send_sem, recv_sem, chunk, per, target).wait_recv()

            for lane in range(per):
                h = part * per + lane
                slot = x * heads + h
                send_buf[slot] = (
                    from_start[rows - 1 : rows, h : h + 1] * recv_buf[slot] + sums[lane]
                )

            @pl.when(me < count - 1)
            def _():
                chunk_copy(send_buf, recv_buf, send_sem, recv_sem, chunk, per, target).start()

            for lane in range(per):
                h = part * per + lane
                slot = x * heads + h
                cut = slice(h * size, (h + 1) * size)
                q = q_ref[x, :, cut]
                state = recv_buf[slot].astype(BF)
                state_ref[slot] = state
                decay = jnp.exp(
                    jnp.where(lower, cols[:, h : h + 1] - row_ref[x, h : h + 1, :], -1e30)
                )
                scores = (mm_nt(q, keys[lane]) * decay).astype(BF)
                outputs = mm(scores, v_ref[x, :, cut]) + from_start[:, h : h + 1] * mm(q, state)
                square = jnp.mean(outputs * outputs, axis=-1, keepdims=True)
                inverse = lax.rsqrt(square + EPSILON) * valid
                normed_ref[x, :, cut] = (outputs * inverse).astype(BF)
                out_ref[x, :, cut] = outputs.astype(BF)
        return carry

    lax.fori_loop(0, tracks, one_track, 0)

    @pl.when(me < count - 1)
    def _():
        def drain(chunk, carry):
            chunk_copy(send_buf, recv_buf, send_sem, recv_sem, chunk, per, target).wait_send()
            return carry

        lax.fori_loop(0, total, drain, 0)


def backward_kernel(
    count, heads, per, q_ref, k_ref, v_ref, col_ref, row_ref, out_ref, gn_ref, state_ref,
    gq_ref, gk_ref, gv_ref, recv_buf, send_buf, send_sem, recv_sem,
):
    me = lax.axis_index("tm")
    tracks, rows, width = q_ref.shape
    size = width // heads
    chunks = heads // per
    total = tracks * chunks
    target = jnp.maximum(me - 1, 0)
    entry_barrier(me, count)

    @pl.when(me == count - 1)
    def _():
        def fill(i, carry):
            recv_buf[pl.ds(i * heads, heads)] = jnp.zeros((heads, size, size), F32)
            return carry

        lax.fori_loop(0, tracks, fill, 0)

    s_index = lax.broadcasted_iota(jnp.int32, (rows, rows), 0)
    t_index = lax.broadcasted_iota(jnp.int32, (rows, rows), 1)
    upper = t_index >= s_index

    def one_track(x, carry):
        cols = col_ref[x]
        valid = cols[:, heads : heads + 1]
        from_start = jnp.exp(cols)
        to_end = jnp.exp(cols[rows - 1 : rows, :] - cols)
        for part in range(chunks):
            chunk = x * chunks + part
            sums = []
            grads = []
            for lane in range(per):
                h = part * per + lane
                cut = slice(h * size, (h + 1) * size)
                outputs = out_ref[x, :, cut].astype(F32)
                square = jnp.mean(outputs * outputs, axis=-1, keepdims=True)
                inverse = lax.rsqrt(square + EPSILON)
                unit = outputs * inverse
                grad = gn_ref[x, :, cut].astype(F32)
                along = jnp.mean(grad * unit, axis=-1, keepdims=True)
                grad = ((inverse * valid) * (grad - unit * along)).astype(BF)
                grads.append(grad)
                q_from = (q_ref[x, :, cut].astype(F32) * from_start[:, h : h + 1]).astype(BF)
                sums.append(mm_tn(q_from, grad))

            @pl.when(me < count - 1)
            def _():
                chunk_copy(send_buf, recv_buf, send_sem, recv_sem, chunk, per, target).wait_recv()

            for lane in range(per):
                h = part * per + lane
                slot = x * heads + h
                send_buf[slot] = (
                    from_start[rows - 1 : rows, h : h + 1] * recv_buf[slot] + sums[lane]
                )

            @pl.when(me > 0)
            def _():
                chunk_copy(send_buf, recv_buf, send_sem, recv_sem, chunk, per, target).start()

            for lane in range(per):
                h = part * per + lane
                slot = x * heads + h
                cut = slice(h * size, (h + 1) * size)
                q = q_ref[x, :, cut]
                v = v_ref[x, :, cut]
                key = (k_ref[x, :, cut].astype(F32) * valid).astype(BF)
                grad = grads[lane]
                end_grad = recv_buf[slot].astype(BF)
                decay = jnp.exp(
                    jnp.where(upper, row_ref[x, h : h + 1, :] - cols[:, h : h + 1], -1e30)
                )
                grad_scores = (mm_nt(v, grad) * decay).astype(BF)
                scores = (mm_nt(key, q) * decay).astype(BF)
                grad_query = mm_tn(grad_scores, key)
                grad_query = grad_query + from_start[:, h : h + 1] * mm_nt(grad, state_ref[slot])
                gq_ref[x, :, cut] = grad_query.astype(BF)
                late = to_end[:, h : h + 1]
                grad_key = mm(grad_scores, q) + late * mm_nt(v, end_grad)
                gk_ref[x, :, cut] = (grad_key * valid).astype(BF)
                grad_value = mm(scores, grad) + late * mm(key, end_grad)
                gv_ref[x, :, cut] = grad_value.astype(BF)
        return carry

    lax.fori_loop(0, tracks, one_track, 0)

    @pl.when(me > 0)
    def _():
        def drain(chunk, carry):
            chunk_copy(send_buf, recv_buf, send_sem, recv_sem, chunk, per, target).wait_send()
            return carry

        lax.fori_loop(0, total, drain, 0)


def cross_kernel(groups, heads, scale, own_ref, bias_ref, *refs):
    q_refs, k_refs, g_refs, n_refs = (refs[i * groups : (i + 1) * groups] for i in range(4))
    outs = refs[4 * groups :]
    gn_outs, gq_outs, gk_outs = (outs[i * groups : (i + 1) * groups] for i in range(3))
    tracks, rows, width = q_refs[0].shape
    size = width // heads
    piece = tracks * rows

    def load(parts, cut):
        return jnp.concatenate([part[:, :, cut].reshape(piece, size) for part in parts], axis=0)

    def store(parts, cut, value):
        for i, part in enumerate(parts):
            part[:, :, cut] = value[i * piece : (i + 1) * piece].astype(BF).reshape(
                tracks, rows, size
            )

    bias = bias_ref[0]
    for h in range(heads):
        cut = slice(h * size, (h + 1) * size)
        q, k, g, n = (load(parts, cut) for parts in (q_refs, k_refs, g_refs, n_refs))
        logits = mm_nt(k, q) * scale + bias
        top = jnp.max(logits, axis=0, keepdims=True)
        weights = jnp.exp(logits - top)
        weights = weights * (1.0 / jnp.sum(weights, axis=0, keepdims=True))
        grad_weights = mm_nt(n, g)
        weighted = weights * grad_weights
        grad_logits = (weighted - weights * jnp.sum(weighted, axis=0, keepdims=True)) * scale
        grad_logits = grad_logits.astype(BF)
        store(gn_outs, cut, mm(weights.astype(BF), g))
        store(gq_outs, cut, mm_tn(grad_logits, k))
        store(gk_outs, cut, mm(grad_logits, q))


def per_device(
    count,
    groups,
    track_query,
    track_key,
    track_value,
    log_decay,
    valid_length,
    initial_state,
    cross_query,
    cross_key,
    grad_out,
):
    tracks, rows, width = track_query.shape
    heads = log_decay.shape[1]
    size = width // heads
    per = HEADS_PER_CHUNK if heads % HEADS_PER_CHUNK == 0 else 1
    chunks = heads // per
    slots = tracks * heads
    all_tracks = valid_length.shape[0]
    mine = lax.axis_index("track")
    time_first = lax.axis_index("tm") * rows
    piece_rows = rows // groups

    grouped = valid_length.reshape(groups, tracks)
    length_of = lambda group: lax.dynamic_index_in_dim(grouped, group, 0, keepdims=False)
    own_length = length_of(mine)
    times = time_first + jnp.arange(rows)
    valid = (times[None, :] < own_length[:, None]).astype(F32)

    triangle = (jnp.arange(rows)[:, None] <= jnp.arange(rows)[None, :]).astype(F32)
    within = jnp.einsum("xhs,st->xht", log_decay, triangle, precision=lax.Precision.HIGHEST)
    cols = jnp.concatenate(
        [
            jnp.transpose(within, (0, 2, 1)),
            valid[:, :, None],
            jnp.zeros((tracks, rows, 128 - heads - 1), F32),
        ],
        axis=2,
    )

    def piece_of(value, group):
        return lax.dynamic_slice_in_dim(value, group * piece_rows, piece_rows, axis=1)

    def send(value, shift):
        perm = [(i, (i + shift) % groups) for i in range(groups)]
        return lax.ppermute(piece_of(value, (mine + shift) % groups), "track", perm)

    grad_masked = grad_out * valid[:, :, None].astype(BF)
    q_parts = [cross_query] + [send(cross_query, s) for s in range(1, groups)]
    k_parts = [cross_key] + [send(cross_key, s) for s in range(1, groups)]
    g_parts = [grad_masked] + [send(grad_masked, s) for s in range(1, groups)]

    vmem = pl.BlockSpec(memory_space=pltpu.VMEM)
    wide = jax.ShapeDtypeStruct((tracks, rows, width), BF)
    scratch = [
        pltpu.VMEM((slots, size, size), F32),
        pltpu.VMEM((slots, size, size), F32),
        pltpu.SemaphoreType.DMA((tracks * chunks,)),
        pltpu.SemaphoreType.DMA((tracks * chunks,)),
    ]
    dot_flops = 2 * slots * rows * size * size
    normed, outputs, states = pl.pallas_call(
        functools.partial(forward_kernel, count, heads, per),
        out_shape=(wide, wide, jax.ShapeDtypeStruct((slots, size, size), BF)),
        in_specs=[vmem] * 6,
        out_specs=(vmem,) * 3,
        scratch_shapes=scratch,
        compiler_params=pltpu.CompilerParams(
            collective_id=0, has_side_effects=True, vmem_limit_bytes=56 * 2**20
        ),
        cost_estimate=pl.CostEstimate(
            flops=400 * dot_flops, bytes_accessed=16 * slots * size * size, transcendentals=0
        ),
        name="forward_chain",
    )(track_query, track_key, track_value, cols, within, initial_state.reshape(slots, size, size))

    n_parts = [normed] + [send(normed, s) for s in range(1, groups)]

    tile = min(16, piece_rows)
    tiles = piece_rows // tile
    lengths = jnp.concatenate([length_of((mine - s) % groups) for s in range(groups)])
    tile_times = (
        time_first + mine * piece_rows + jnp.arange(piece_rows).reshape(tiles, 1, tile)
    )
    key_valid = (tile_times < lengths[None, :, None]).reshape(tiles, all_tracks * tile, 1)
    row_time = jnp.arange(all_tracks * tile) % tile
    same_time = row_time[:, None] == row_time[None, :]
    bias = jnp.where(key_valid & same_time[None], 0.0, -1e30).astype(F32)
    own_block = jnp.reshape(mine * tiles, (1,)).astype(jnp.int32)

    own_spec = pl.BlockSpec((tracks, tile, width), lambda t, own: (0, own[0] + t, 0))
    other_spec = pl.BlockSpec((tracks, tile, width), lambda t, own: (0, t, 0))
    bias_spec = pl.BlockSpec(
        (1, all_tracks * tile, all_tracks * tile), lambda t, own: (t, 0, 0)
    )
    piece_shape = jax.ShapeDtypeStruct((tracks, piece_rows, width), BF)
    cross = pl.pallas_call(
        functools.partial(cross_kernel, groups, heads, 1.0 / float(size) ** 0.5),
        out_shape=(piece_shape,) * (3 * groups),
        grid_spec=pltpu.PrefetchScalarGridSpec(
            num_scalar_prefetch=1,
            grid=(tiles,),
            in_specs=[bias_spec] + ([own_spec] + [other_spec] * (groups - 1)) * 4,
            out_specs=(other_spec,) * (3 * groups),
        ),
        compiler_params=pltpu.CompilerParams(vmem_limit_bytes=56 * 2**20),
        cost_estimate=pl.CostEstimate(
            flops=100 * dot_flops, bytes_accessed=16 * slots * size * size, transcendentals=0
        ),
        name="cross_attention",
    )(own_block, bias, *q_parts, *k_parts, *g_parts, *n_parts)

    def collect(parts):
        whole = jnp.zeros((tracks, rows, width), BF)
        for s, part in enumerate(parts):
            if s:
                perm = [(i, (i - s) % groups) for i in range(groups)]
                part = lax.ppermute(part, "track", perm)
            start = ((mine + s) % groups) * piece_rows
            whole = lax.dynamic_update_slice_in_dim(whole, part, start, axis=1)
        return whole

    grad_normed = collect(cross[:groups])
    grad_cross_query = collect(cross[groups : 2 * groups])
    grad_cross_key = collect(cross[2 * groups :])

    grad_query, grad_key, grad_value = pl.pallas_call(
        functools.partial(backward_kernel, count, heads, per),
        out_shape=(wide,) * 3,
        in_specs=[vmem] * 8,
        out_specs=(vmem,) * 3,
        scratch_shapes=scratch,
        compiler_params=pltpu.CompilerParams(
            collective_id=1, has_side_effects=True, vmem_limit_bytes=60 * 2**20
        ),
        cost_estimate=pl.CostEstimate(
            flops=400 * dot_flops, bytes_accessed=16 * slots * size * size, transcendentals=0
        ),
        name="backward_chain",
    )(track_query, track_key, track_value, cols, within, outputs, grad_normed, states)
    return grad_query, grad_key, grad_value, grad_cross_query, grad_cross_key


def solution(mesh):
    wide = P("track", "tm", None)
    return jax.shard_map(
        functools.partial(per_device, mesh.shape["tm"], mesh.shape["track"]),
        mesh=mesh,
        in_specs=(
            wide,
            wide,
            wide,
            P("track", None, "tm"),
            P(),
            P("track", None, None, None),
            wide,
            wide,
            wide,
        ),
        out_specs=(wide,) * 5,
        check_vma=False,
    )
```

```python
import functools

import jax
import jax.numpy as jnp
from jax import lax
from jax.experimental import pallas as pl
from jax.experimental.pallas import tpu as pltpu
from jax.sharding import PartitionSpec as P


EPSILON = 1e-06
MESH = pl.DeviceIdType.MESH
BF = jnp.bfloat16
F32 = jnp.float32
HEADS_PER_CHUNK = 1
PARTS = 2


def mm(a, b):
    return lax.dot_general(a, b, (((1,), (0,)), ((), ())), preferred_element_type=F32)


def mm_nt(a, b):
    return lax.dot_general(a, b, (((1,), (1,)), ((), ())), preferred_element_type=F32)


def mm_tn(a, b):
    return lax.dot_general(a, b, (((0,), (0,)), ((), ())), preferred_element_type=F32)


def entry_barrier(me, count):
    barrier = pltpu.get_barrier_semaphore()

    @pl.when(me > 0)
    def _():
        pl.semaphore_signal(barrier, inc=1, device_id={"tm": me - 1}, device_id_type=MESH)

    @pl.when(me < count - 1)
    def _():
        pl.semaphore_signal(barrier, inc=1, device_id={"tm": me + 1}, device_id_type=MESH)

    peers = jnp.where(me > 0, 1, 0) + jnp.where(me < count - 1, 1, 0)
    pl.semaphore_wait(barrier, peers)


def chunk_copy(send_buf, recv_buf, send_sem, recv_sem, chunk, per, target):
    return pltpu.make_async_remote_copy(
        src_ref=send_buf.at[pl.ds(chunk * per, per)],
        dst_ref=recv_buf.at[pl.ds(chunk * per, per)],
        send_sem=send_sem.at[chunk],
        recv_sem=recv_sem.at[chunk],
        device_id={"tm": target},
        device_id_type=MESH,
    )


def split(value):
    high = value.astype(BF)
    return high, (value - high.astype(F32)).astype(BF)


def forward_kernel(
    count, heads, first, lanes, per, q_ref, k_ref, v_ref, col_ref, row_ref, init_ref,
    normed_ref, out_ref, state_ref, recv_buf, send_buf, send_sem, recv_sem,
):
    me = lax.axis_index("tm")
    tracks, rows, width = q_ref.shape
    size = width // heads
    chunks = heads // per
    total = tracks * chunks
    target = jnp.minimum(me + 1, count - 1)
    entry_barrier(me, count)

    @pl.when(me == 0)
    def _():
        def fill(i, carry):
            recv_buf[pl.ds(i * heads, heads)] = init_ref[i].astype(F32)
            return carry

        lax.fori_loop(0, tracks, fill, 0)

    t_index = lax.broadcasted_iota(jnp.int32, (rows, rows), 0)
    s_index = lax.broadcasted_iota(jnp.int32, (rows, rows), 1)
    lower = t_index >= s_index

    def one_track(x, carry):
        cols = col_ref[x]
        valid = cols[:, lanes : lanes + 1]
        from_start = jnp.exp(cols)
        to_end = jnp.exp(cols[rows - 1 : rows, :] - cols)
        for part in range(chunks):
            chunk = x * chunks + part
            sums = []
            keys = []
            for lane in range(per):
                h = part * per + lane
                cut = slice(h * size, (h + 1) * size)
                k_float = k_ref[x, :, cut].astype(F32) * valid
                keys.append(k_float.astype(BF))
                high, low = split(k_float * to_end[:, first + h : first + h + 1])
                v = v_ref[x, :, cut]
                sums.append(mm_tn(high, v) + mm_tn(low, v))

            @pl.when(me > 0)
            def _():
                chunk_copy(send_buf, recv_buf, send_sem, recv_sem, chunk, per, target).wait_recv()

            for lane in range(per):
                h = part * per + lane
                slot = x * heads + h
                send_buf[slot] = (
                    from_start[rows - 1 : rows, first + h : first + h + 1] * recv_buf[slot] + sums[lane]
                )

            @pl.when(me < count - 1)
            def _():
                chunk_copy(send_buf, recv_buf, send_sem, recv_sem, chunk, per, target).start()

            for lane in range(per):
                h = part * per + lane
                slot = x * heads + h
                cut = slice(h * size, (h + 1) * size)
                q = q_ref[x, :, cut]
                state, state_low = split(recv_buf[slot])
                state_ref[slot] = state
                decay = jnp.exp(
                    jnp.where(lower, cols[:, first + h : first + h + 1] - row_ref[x, first + h : first + h + 1, :], -1e30)
                )
                scores, scores_low = split(mm_nt(q, keys[lane]) * decay)
                v = v_ref[x, :, cut]
                late = mm(q, state) + mm(q, state_low)
                outputs = mm(scores, v) + mm(scores_low, v)
                outputs = outputs + from_start[:, first + h : first + h + 1] * late
                square = jnp.mean(outputs * outputs, axis=-1, keepdims=True)
                inverse = lax.rsqrt(square + EPSILON) * valid
                normed_ref[x, :, cut] = (outputs * inverse).astype(BF)
                out_ref[x, :, cut] = outputs.astype(BF)
        return carry

    lax.fori_loop(0, tracks, one_track, 0)

    @pl.when(me < count - 1)
    def _():
        def drain(chunk, carry):
            chunk_copy(send_buf, recv_buf, send_sem, recv_sem, chunk, per, target).wait_send()
            return carry

        lax.fori_loop(0, total, drain, 0)


def backward_kernel(
    count, heads, first, lanes, per, q_ref, k_ref, v_ref, col_ref, row_ref, out_ref, gn_ref, state_ref,
    gq_ref, gk_ref, gv_ref, recv_buf, send_buf, send_sem, recv_sem,
):
    me = lax.axis_index("tm")
    tracks, rows, width = q_ref.shape
    size = width // heads
    chunks = heads // per
    total = tracks * chunks
    target = jnp.maximum(me - 1, 0)
    entry_barrier(me, count)

    @pl.when(me == count - 1)
    def _():
        def fill(i, carry):
            recv_buf[pl.ds(i * heads, heads)] = jnp.zeros((heads, size, size), F32)
            return carry

        lax.fori_loop(0, tracks, fill, 0)

    s_index = lax.broadcasted_iota(jnp.int32, (rows, rows), 0)
    t_index = lax.broadcasted_iota(jnp.int32, (rows, rows), 1)
    upper = t_index >= s_index

    def one_track(x, carry):
        cols = col_ref[x]
        valid = cols[:, lanes : lanes + 1]
        from_start = jnp.exp(cols)
        to_end = jnp.exp(cols[rows - 1 : rows, :] - cols)
        for part in range(chunks):
            chunk = x * chunks + part
            sums = []
            grads = []
            for lane in range(per):
                h = part * per + lane
                cut = slice(h * size, (h + 1) * size)
                outputs = out_ref[x, :, cut].astype(F32)
                square = jnp.mean(outputs * outputs, axis=-1, keepdims=True)
                inverse = lax.rsqrt(square + EPSILON)
                unit = outputs * inverse
                grad = gn_ref[x, :, cut].astype(F32)
                along = jnp.mean(grad * unit, axis=-1, keepdims=True)
                grad = ((inverse * valid) * (grad - unit * along)).astype(BF)
                grads.append(grad)
                q_from = (q_ref[x, :, cut].astype(F32) * from_start[:, first + h : first + h + 1]).astype(BF)
                sums.append(mm_tn(q_from, grad))

            @pl.when(me < count - 1)
            def _():
                chunk_copy(send_buf, recv_buf, send_sem, recv_sem, chunk, per, target).wait_recv()

            for lane in range(per):
                h = part * per + lane
                slot = x * heads + h
                send_buf[slot] = (
                    from_start[rows - 1 : rows, first + h : first + h + 1] * recv_buf[slot] + sums[lane]
                )

            @pl.when(me > 0)
            def _():
                chunk_copy(send_buf, recv_buf, send_sem, recv_sem, chunk, per, target).start()

            for lane in range(per):
                h = part * per + lane
                slot = x * heads + h
                cut = slice(h * size, (h + 1) * size)
                q = q_ref[x, :, cut]
                v = v_ref[x, :, cut]
                key = (k_ref[x, :, cut].astype(F32) * valid).astype(BF)
                grad = grads[lane]
                end_grad = recv_buf[slot].astype(BF)
                decay = jnp.exp(
                    jnp.where(upper, row_ref[x, first + h : first + h + 1, :] - cols[:, first + h : first + h + 1], -1e30)
                )
                grad_scores = (mm_nt(v, grad) * decay).astype(BF)
                scores = (mm_nt(key, q) * decay).astype(BF)
                grad_query = mm_tn(grad_scores, key)
                grad_query = grad_query + from_start[:, first + h : first + h + 1] * mm_nt(grad, state_ref[slot])
                gq_ref[x, :, cut] = grad_query.astype(BF)
                late = to_end[:, first + h : first + h + 1]
                grad_key = mm(grad_scores, q) + late * mm_nt(v, end_grad)
                gk_ref[x, :, cut] = (grad_key * valid).astype(BF)
                grad_value = mm(scores, grad) + late * mm(key, end_grad)
                gv_ref[x, :, cut] = grad_value.astype(BF)
        return carry

    lax.fori_loop(0, tracks, one_track, 0)

    @pl.when(me > 0)
    def _():
        def drain(chunk, carry):
            chunk_copy(send_buf, recv_buf, send_sem, recv_sem, chunk, per, target).wait_send()
            return carry

        lax.fori_loop(0, total, drain, 0)


def cross_kernel(groups, heads, scale, own_ref, bias_ref, *refs):
    q_refs, k_refs, g_refs, n_refs = (refs[i * groups : (i + 1) * groups] for i in range(4))
    outs = refs[4 * groups :]
    gn_outs, gq_outs, gk_outs = (outs[i * groups : (i + 1) * groups] for i in range(3))
    tracks, rows, width = q_refs[0].shape
    size = width // heads
    piece = tracks * rows

    def load(parts, cut):
        return jnp.concatenate([part[:, :, cut].reshape(piece, size) for part in parts], axis=0)

    def store(parts, cut, value):
        for i, part in enumerate(parts):
            part[:, :, cut] = value[i * piece : (i + 1) * piece].astype(BF).reshape(
                tracks, rows, size
            )

    bias = bias_ref[0]
    for h in range(heads):
        cut = slice(h * size, (h + 1) * size)
        q, k, g, n = (load(parts, cut) for parts in (q_refs, k_refs, g_refs, n_refs))
        logits = mm_nt(k, q) * scale + bias
        top = jnp.max(logits, axis=0, keepdims=True)
        weights = jnp.exp(logits - top)
        weights = weights * (1.0 / jnp.sum(weights, axis=0, keepdims=True))
        grad_weights = mm_nt(n, g)
        weighted = weights * grad_weights
        grad_logits = (weighted - weights * jnp.sum(weighted, axis=0, keepdims=True)) * scale
        grad_logits = grad_logits.astype(BF)
        store(gn_outs, cut, mm(weights.astype(BF), g))
        store(gq_outs, cut, mm_tn(grad_logits, k))
        store(gk_outs, cut, mm(grad_logits, q))


def per_device(
    count,
    groups,
    track_query,
    track_key,
    track_value,
    log_decay,
    valid_length,
    initial_state,
    cross_query,
    cross_key,
    grad_out,
):
    tracks, rows, width = track_query.shape
    heads = log_decay.shape[1]
    size = width // heads
    parts = PARTS if heads % PARTS == 0 else 1
    part_heads = heads // parts
    part_width = width // parts
    per = HEADS_PER_CHUNK if part_heads % HEADS_PER_CHUNK == 0 else 1
    chunks = part_heads // per
    slots = tracks * part_heads
    all_tracks = valid_length.shape[0]
    mine = lax.axis_index("track")
    time_first = lax.axis_index("tm") * rows
    piece_rows = rows // groups

    grouped = valid_length.reshape(groups, tracks)
    length_of = lambda group: lax.dynamic_index_in_dim(grouped, group, 0, keepdims=False)
    own_length = length_of(mine)
    times = time_first + jnp.arange(rows)
    valid = (times[None, :] < own_length[:, None]).astype(F32)

    triangle = (jnp.arange(rows)[:, None] <= jnp.arange(rows)[None, :]).astype(F32)
    within = jnp.einsum("xhs,st->xht", log_decay, triangle, precision=lax.Precision.HIGHEST)
    cols = jnp.concatenate(
        [
            jnp.transpose(within, (0, 2, 1)),
            valid[:, :, None],
            jnp.zeros((tracks, rows, 128 - heads - 1), F32),
        ],
        axis=2,
    )

    def send(value, shift):
        perm = [(i, (i + shift) % groups) for i in range(groups)]
        start = ((mine + shift) % groups) * piece_rows
        piece = lax.dynamic_slice_in_dim(value, start, piece_rows, axis=1)
        return lax.ppermute(piece, "track", perm)

    grad_masked = grad_out * valid[:, :, None].astype(BF)
    q_parts = [cross_query] + [send(cross_query, s) for s in range(1, groups)]
    k_parts = [cross_key] + [send(cross_key, s) for s in range(1, groups)]
    g_parts = [grad_masked] + [send(grad_masked, s) for s in range(1, groups)]

    once = pl.Buffered(1)

    def wide_spec(part):
        return pl.BlockSpec(
            (tracks, rows, part_width), lambda i: (0, 0, part), pipeline_mode=once
        )

    narrow_spec = wide_spec(0)
    col_spec = pl.BlockSpec((tracks, rows, 128), lambda i: (0, 0, 0), pipeline_mode=once)
    row_spec = pl.BlockSpec((tracks, heads, rows), lambda i: (0, 0, 0), pipeline_mode=once)
    state_spec = pl.BlockSpec((slots, size, size), lambda i: (0, 0, 0), pipeline_mode=once)
    narrow = jax.ShapeDtypeStruct((tracks, rows, part_width), BF)
    scratch = [
        pltpu.VMEM((slots, size, size), F32),
        pltpu.VMEM((slots, size, size), F32),
        pltpu.SemaphoreType.DMA((tracks * chunks,)),
        pltpu.SemaphoreType.DMA((tracks * chunks,)),
    ]
    dot_flops = 2 * slots * rows * size * size

    def estimate(times_over):
        return pl.CostEstimate(
            flops=times_over * dot_flops,
            bytes_accessed=16 * slots * size * size,
            transcendentals=0,
        )

    forward = []
    for part in range(parts):
        init_spec = pl.BlockSpec(
            (tracks, part_heads, size, size),
            functools.partial(lambda part, i: (0, part, 0, 0), part),
            pipeline_mode=once,
        )
        forward.append(
            pl.pallas_call(
                functools.partial(forward_kernel, count, part_heads, part * part_heads, heads, per),
                out_shape=(narrow, narrow, jax.ShapeDtypeStruct((slots, size, size), BF)),
                grid=(1,),
                in_specs=[wide_spec(part)] * 3 + [col_spec, row_spec, init_spec],
                out_specs=(narrow_spec, narrow_spec, state_spec),
                scratch_shapes=scratch,
                compiler_params=pltpu.CompilerParams(
                    collective_id=part,
                    has_side_effects=True,
                    vmem_limit_bytes=48 * 2**20,
                ),
                cost_estimate=estimate(400),
            )(track_query, track_key, track_value, cols, within, initial_state)
        )

    tile = min(16, piece_rows)
    tiles = piece_rows // tile
    lengths = jnp.concatenate([length_of((mine - s) % groups) for s in range(groups)])
    tile_times = (
        time_first + mine * piece_rows + jnp.arange(piece_rows).reshape(tiles, 1, tile)
    )
    key_valid = (tile_times < lengths[None, :, None]).reshape(tiles, all_tracks * tile, 1)
    row_time = jnp.arange(all_tracks * tile) % tile
    same_time = row_time[:, None] == row_time[None, :]
    bias = jnp.where(key_valid & same_time[None], 0.0, -1e30).astype(F32)
    own_block = jnp.reshape(mine * tiles, (1,)).astype(jnp.int32)
    bias_spec = pl.BlockSpec(
        (1, all_tracks * tile, all_tracks * tile), lambda t, own: (t, 0, 0)
    )
    result_spec = pl.BlockSpec((tracks, tile, part_width), lambda t, own: (0, t, 0))
    piece_shape = jax.ShapeDtypeStruct((tracks, piece_rows, part_width), BF)

    back_perms = [[(i, (i - s) % groups) for i in range(groups)] for s in range(groups)]

    def returned(pieces):
        return [
            lax.ppermute(piece, "track", back_perms[s]) if s else piece
            for s, piece in enumerate(pieces)
        ]

    n_all = []
    for part in range(parts):
        normed = forward[part][0]
        n_all.append([normed] + [send(normed, s) for s in range(1, groups)])

    gn_all, gq_all, gk_all = [], [], []
    for part in range(parts):
        own_spec = pl.BlockSpec(
            (tracks, tile, part_width),
            functools.partial(lambda part, t, own: (0, own[0] + t, part), part),
        )
        other_spec = pl.BlockSpec(
            (tracks, tile, part_width), functools.partial(lambda part, t, own: (0, t, part), part)
        )
        own_normed = pl.BlockSpec(
            (tracks, tile, part_width), lambda t, own: (0, own[0] + t, 0)
        )
        cross = pl.pallas_call(
            functools.partial(cross_kernel, groups, part_heads, 1.0 / float(size) ** 0.5),
            out_shape=(piece_shape,) * (3 * groups),
            grid_spec=pltpu.PrefetchScalarGridSpec(
                num_scalar_prefetch=1,
                grid=(tiles,),
                in_specs=[bias_spec]
                + ([own_spec] + [other_spec] * (groups - 1)) * 3
                + [own_normed]
                + [result_spec] * (groups - 1),
                out_specs=(result_spec,) * (3 * groups),
            ),
            compiler_params=pltpu.CompilerParams(vmem_limit_bytes=48 * 2**20),
            cost_estimate=estimate(100),
        )(own_block, bias, *q_parts, *k_parts, *g_parts, *n_all[part])
        gn_all.append(returned(cross[:groups]))
        gq_all.append(returned(cross[groups : 2 * groups]))
        gk_all.append(returned(cross[2 * groups :]))

    def collect(all_pieces, whole_width):
        whole = jnp.zeros((tracks, rows, whole_width), BF)
        for part, pieces in enumerate(all_pieces):
            for s, piece in enumerate(pieces):
                start = ((mine + s) % groups) * piece_rows
                whole = lax.dynamic_update_slice(whole, piece, (0, start, part * part_width))
        return whole

    backward = []
    for part in range(parts):
        grad_normed = collect(gn_all[part : part + 1], part_width)
        backward.append(
            pl.pallas_call(
                functools.partial(
                    backward_kernel, count, part_heads, part * part_heads, heads, per
                ),
                out_shape=(narrow,) * 3,
                grid=(1,),
                in_specs=[wide_spec(part)] * 3
                + [col_spec, row_spec, narrow_spec, narrow_spec, state_spec],
                out_specs=(narrow_spec,) * 3,
                scratch_shapes=scratch,
                compiler_params=pltpu.CompilerParams(
                    collective_id=parts + part,
                    has_side_effects=True,
                    vmem_limit_bytes=48 * 2**20,
                ),
                cost_estimate=estimate(400),
            )(
                track_query,
                track_key,
                track_value,
                cols,
                within,
                forward[part][1],
                grad_normed,
                forward[part][2],
            )
        )

    grads = [
        jnp.concatenate([backward[part][i] for part in range(parts)], axis=2) for i in range(3)
    ]
    return grads[0], grads[1], grads[2], collect(gq_all, width), collect(gk_all, width)


def solution(mesh):
    wide = P("track", "tm", None)
    return jax.shard_map(
        functools.partial(per_device, mesh.shape["tm"], mesh.shape["track"]),
        mesh=mesh,
        in_specs=(
            wide,
            wide,
            wide,
            P("track", None, "tm"),
            P(),
            P("track", None, None, None),
            wide,
            wide,
            wide,
        ),
        out_specs=(wide,) * 5,
        check_vma=False,
    )
```

```python
import functools

import jax
import jax.numpy as jnp
from jax import lax
from jax.experimental import pallas as pl
from jax.experimental.pallas import tpu as pltpu
from jax.sharding import PartitionSpec as P


EPSILON = 1e-06
MESH = pl.DeviceIdType.MESH
BF = jnp.bfloat16
F32 = jnp.float32
HEADS_PER_CHUNK = 1
PARTS = 2


def mm(a, b):
    return lax.dot_general(a, b, (((1,), (0,)), ((), ())), preferred_element_type=F32)


def mm_nt(a, b):
    return lax.dot_general(a, b, (((1,), (1,)), ((), ())), preferred_element_type=F32)


def mm_tn(a, b):
    return lax.dot_general(a, b, (((0,), (0,)), ((), ())), preferred_element_type=F32)


def entry_barrier(me, count):
    barrier = pltpu.get_barrier_semaphore()

    @pl.when(me > 0)
    def _():
        pl.semaphore_signal(barrier, inc=1, device_id={"tm": me - 1}, device_id_type=MESH)

    @pl.when(me < count - 1)
    def _():
        pl.semaphore_signal(barrier, inc=1, device_id={"tm": me + 1}, device_id_type=MESH)

    peers = jnp.where(me > 0, 1, 0) + jnp.where(me < count - 1, 1, 0)
    pl.semaphore_wait(barrier, peers)


def chunk_copy(send_buf, recv_buf, send_sem, recv_sem, chunk, per, target):
    return pltpu.make_async_remote_copy(
        src_ref=send_buf.at[pl.ds(chunk * per, per)],
        dst_ref=recv_buf.at[pl.ds(chunk * per, per)],
        send_sem=send_sem.at[chunk],
        recv_sem=recv_sem.at[chunk],
        device_id={"tm": target},
        device_id_type=MESH,
    )


def split(value):
    high = value.astype(BF)
    return high, (value - high.astype(F32)).astype(BF)


def forward_kernel(
    count, heads, first, lanes, per, q_ref, k_ref, v_ref, col_ref, row_ref, init_ref,
    normed_ref, out_ref, state_ref, recv_buf, send_buf, send_sem, recv_sem,
):
    me = lax.axis_index("tm")
    tracks, rows, width = q_ref.shape
    size = width // heads
    chunks = heads // per
    total = tracks * chunks
    target = jnp.minimum(me + 1, count - 1)
    entry_barrier(me, count)

    @pl.when(me == 0)
    def _():
        def fill(i, carry):
            recv_buf[pl.ds(i * heads, heads)] = init_ref[i].astype(F32)
            return carry

        lax.fori_loop(0, tracks, fill, 0)

    t_index = lax.broadcasted_iota(jnp.int32, (rows, rows), 0)
    s_index = lax.broadcasted_iota(jnp.int32, (rows, rows), 1)
    lower = t_index >= s_index

    def one_track(x, carry):
        cols = col_ref[x]
        valid = cols[:, lanes : lanes + 1]
        from_start = jnp.exp(cols)
        to_end = jnp.exp(cols[rows - 1 : rows, :] - cols)
        for part in range(chunks):
            chunk = x * chunks + part
            sums = []
            keys = []
            for lane in range(per):
                h = part * per + lane
                cut = slice(h * size, (h + 1) * size)
                k_float = k_ref[x, :, cut].astype(F32) * valid
                keys.append(k_float.astype(BF))
                high, low = split(k_float * to_end[:, first + h : first + h + 1])
                v = v_ref[x, :, cut]
                sums.append(mm_tn(high, v) + mm_tn(low, v))

            @pl.when(me > 0)
            def _():
                chunk_copy(send_buf, recv_buf, send_sem, recv_sem, chunk, per, target).wait_recv()

            for lane in range(per):
                h = part * per + lane
                slot = x * heads + h
                send_buf[slot] = (
                    from_start[rows - 1 : rows, first + h : first + h + 1] * recv_buf[slot] + sums[lane]
                )

            @pl.when(me < count - 1)
            def _():
                chunk_copy(send_buf, recv_buf, send_sem, recv_sem, chunk, per, target).start()

            for lane in range(per):
                h = part * per + lane
                slot = x * heads + h
                cut = slice(h * size, (h + 1) * size)
                q = q_ref[x, :, cut]
                state, state_low = split(recv_buf[slot])
                state_ref[slot] = state
                decay = jnp.exp(
                    jnp.where(lower, cols[:, first + h : first + h + 1] - row_ref[x, first + h : first + h + 1, :], -1e30)
                )
                scores, scores_low = split(mm_nt(q, keys[lane]) * decay)
                v = v_ref[x, :, cut]
                late = mm(q, state) + mm(q, state_low)
                outputs = mm(scores, v) + mm(scores_low, v)
                outputs = outputs + from_start[:, first + h : first + h + 1] * late
                square = jnp.mean(outputs * outputs, axis=-1, keepdims=True)
                inverse = lax.rsqrt(square + EPSILON) * valid
                normed_ref[x, :, cut] = (outputs * inverse).astype(BF)
                out_ref[x, :, cut] = outputs.astype(BF)
        return carry

    lax.fori_loop(0, tracks, one_track, 0)

    @pl.when(me < count - 1)
    def _():
        def drain(chunk, carry):
            chunk_copy(send_buf, recv_buf, send_sem, recv_sem, chunk, per, target).wait_send()
            return carry

        lax.fori_loop(0, total, drain, 0)


def backward_kernel(
    count, heads, first, lanes, per, q_ref, k_ref, v_ref, col_ref, row_ref, out_ref, gn_ref, state_ref,
    gq_ref, gk_ref, gv_ref, recv_buf, send_buf, send_sem, recv_sem,
):
    me = lax.axis_index("tm")
    tracks, rows, width = q_ref.shape
    size = width // heads
    chunks = heads // per
    total = tracks * chunks
    target = jnp.maximum(me - 1, 0)
    entry_barrier(me, count)

    @pl.when(me == count - 1)
    def _():
        def fill(i, carry):
            recv_buf[pl.ds(i * heads, heads)] = jnp.zeros((heads, size, size), F32)
            return carry

        lax.fori_loop(0, tracks, fill, 0)

    s_index = lax.broadcasted_iota(jnp.int32, (rows, rows), 0)
    t_index = lax.broadcasted_iota(jnp.int32, (rows, rows), 1)
    upper = t_index >= s_index

    def one_track(x, carry):
        cols = col_ref[x]
        valid = cols[:, lanes : lanes + 1]
        from_start = jnp.exp(cols)
        to_end = jnp.exp(cols[rows - 1 : rows, :] - cols)
        for part in range(chunks):
            chunk = x * chunks + part
            sums = []
            grads = []
            for lane in range(per):
                h = part * per + lane
                cut = slice(h * size, (h + 1) * size)
                outputs = out_ref[x, :, cut].astype(F32)
                square = jnp.mean(outputs * outputs, axis=-1, keepdims=True)
                inverse = lax.rsqrt(square + EPSILON)
                unit = outputs * inverse
                grad = gn_ref[x, :, cut].astype(F32)
                along = jnp.mean(grad * unit, axis=-1, keepdims=True)
                grad = ((inverse * valid) * (grad - unit * along)).astype(BF)
                grads.append(grad)
                q_from = (q_ref[x, :, cut].astype(F32) * from_start[:, first + h : first + h + 1]).astype(BF)
                sums.append(mm_tn(q_from, grad))

            @pl.when(me < count - 1)
            def _():
                chunk_copy(send_buf, recv_buf, send_sem, recv_sem, chunk, per, target).wait_recv()

            for lane in range(per):
                h = part * per + lane
                slot = x * heads + h
                send_buf[slot] = (
                    from_start[rows - 1 : rows, first + h : first + h + 1] * recv_buf[slot] + sums[lane]
                )

            @pl.when(me > 0)
            def _():
                chunk_copy(send_buf, recv_buf, send_sem, recv_sem, chunk, per, target).start()

            for lane in range(per):
                h = part * per + lane
                slot = x * heads + h
                cut = slice(h * size, (h + 1) * size)
                q = q_ref[x, :, cut]
                v = v_ref[x, :, cut]
                key = (k_ref[x, :, cut].astype(F32) * valid).astype(BF)
                grad = grads[lane]
                end_grad = recv_buf[slot].astype(BF)
                decay = jnp.exp(
                    jnp.where(upper, row_ref[x, first + h : first + h + 1, :] - cols[:, first + h : first + h + 1], -1e30)
                )
                grad_scores = (mm_nt(v, grad) * decay).astype(BF)
                scores = (mm_nt(key, q) * decay).astype(BF)
                grad_query = mm_tn(grad_scores, key)
                grad_query = grad_query + from_start[:, first + h : first + h + 1] * mm_nt(grad, state_ref[slot])
                gq_ref[x, :, cut] = grad_query.astype(BF)
                late = to_end[:, first + h : first + h + 1]
                grad_key = mm(grad_scores, q) + late * mm_nt(v, end_grad)
                gk_ref[x, :, cut] = (grad_key * valid).astype(BF)
                grad_value = mm(scores, grad) + late * mm(key, end_grad)
                gv_ref[x, :, cut] = grad_value.astype(BF)
        return carry

    lax.fori_loop(0, tracks, one_track, 0)

    @pl.when(me > 0)
    def _():
        def drain(chunk, carry):
            chunk_copy(send_buf, recv_buf, send_sem, recv_sem, chunk, per, target).wait_send()
            return carry

        lax.fori_loop(0, total, drain, 0)


def cross_kernel(groups, heads, scale, own_ref, bias_ref, *refs):
    q_refs, k_refs, g_refs, n_refs = (refs[i * groups : (i + 1) * groups] for i in range(4))
    outs = refs[4 * groups :]
    gn_outs, gq_outs, gk_outs = (outs[i * groups : (i + 1) * groups] for i in range(3))
    tracks, rows, width = q_refs[0].shape
    size = width // heads
    piece = tracks * rows

    def load(parts, cut):
        return jnp.concatenate([part[:, :, cut].reshape(piece, size) for part in parts], axis=0)

    def store(parts, cut, value):
        for i, part in enumerate(parts):
            part[:, :, cut] = value[i * piece : (i + 1) * piece].astype(BF).reshape(
                tracks, rows, size
            )

    bias = bias_ref[0]
    for h in range(heads):
        cut = slice(h * size, (h + 1) * size)
        q, k, g, n = (load(parts, cut) for parts in (q_refs, k_refs, g_refs, n_refs))
        logits = mm_nt(k, q) * scale + bias
        top = jnp.max(logits, axis=0, keepdims=True)
        weights = jnp.exp(logits - top)
        weights = weights * (1.0 / jnp.sum(weights, axis=0, keepdims=True))
        grad_weights = mm_nt(n, g)
        weighted = weights * grad_weights
        grad_logits = (weighted - weights * jnp.sum(weighted, axis=0, keepdims=True)) * scale
        grad_logits = grad_logits.astype(BF)
        store(gn_outs, cut, mm(weights.astype(BF), g))
        store(gq_outs, cut, mm_tn(grad_logits, k))
        store(gk_outs, cut, mm(grad_logits, q))


def per_device(
    count,
    groups,
    track_query,
    track_key,
    track_value,
    log_decay,
    valid_length,
    initial_state,
    cross_query,
    cross_key,
    grad_out,
):
    tracks, rows, width = track_query.shape
    heads = log_decay.shape[1]
    size = width // heads
    parts = PARTS if heads % PARTS == 0 else 1
    part_heads = heads // parts
    part_width = width // parts
    per = HEADS_PER_CHUNK if part_heads % HEADS_PER_CHUNK == 0 else 1
    chunks = part_heads // per
    slots = tracks * part_heads
    all_tracks = valid_length.shape[0]
    mine = lax.axis_index("track")
    time_first = lax.axis_index("tm") * rows
    piece_rows = rows // groups

    grouped = valid_length.reshape(groups, tracks)
    length_of = lambda group: lax.dynamic_index_in_dim(grouped, group, 0, keepdims=False)
    own_length = length_of(mine)
    times = time_first + jnp.arange(rows)
    valid = (times[None, :] < own_length[:, None]).astype(F32)

    triangle = (jnp.arange(rows)[:, None] <= jnp.arange(rows)[None, :]).astype(F32)
    within = jnp.einsum("xhs,st->xht", log_decay, triangle, precision=lax.Precision.HIGHEST)
    cols = jnp.concatenate(
        [
            jnp.transpose(within, (0, 2, 1)),
            valid[:, :, None],
            jnp.zeros((tracks, rows, 128 - heads - 1), F32),
        ],
        axis=2,
    )

    def send(value, shift):
        perm = [(i, (i + shift) % groups) for i in range(groups)]
        start = ((mine + shift) % groups) * piece_rows
        piece = lax.dynamic_slice_in_dim(value, start, piece_rows, axis=1)
        return lax.ppermute(piece, "track", perm)

    grad_masked = grad_out * valid[:, :, None].astype(BF)
    q_parts = [cross_query] + [send(cross_query, s) for s in range(1, groups)]
    k_parts = [cross_key] + [send(cross_key, s) for s in range(1, groups)]
    g_parts = [grad_masked] + [send(grad_masked, s) for s in range(1, groups)]

    once = pl.Buffered(1)

    def wide_spec(part):
        return pl.BlockSpec(
            (tracks, rows, part_width), lambda i: (0, 0, part), pipeline_mode=once
        )

    narrow_spec = wide_spec(0)
    col_spec = pl.BlockSpec((tracks, rows, 128), lambda i: (0, 0, 0), pipeline_mode=once)
    row_spec = pl.BlockSpec((tracks, heads, rows), lambda i: (0, 0, 0), pipeline_mode=once)
    state_spec = pl.BlockSpec((slots, size, size), lambda i: (0, 0, 0), pipeline_mode=once)
    narrow = jax.ShapeDtypeStruct((tracks, rows, part_width), BF)
    scratch = [
        pltpu.VMEM((slots, size, size), F32),
        pltpu.VMEM((slots, size, size), F32),
        pltpu.SemaphoreType.DMA((tracks * chunks,)),
        pltpu.SemaphoreType.DMA((tracks * chunks,)),
    ]
    dot_flops = 2 * slots * rows * size * size

    def estimate(times_over):
        return pl.CostEstimate(
            flops=times_over * dot_flops,
            bytes_accessed=16 * slots * size * size,
            transcendentals=0,
        )

    forward = []
    for part in range(parts):
        init_spec = pl.BlockSpec(
            (tracks, part_heads, size, size),
            functools.partial(lambda part, i: (0, part, 0, 0), part),
            pipeline_mode=once,
        )
        forward.append(
            pl.pallas_call(
                functools.partial(forward_kernel, count, part_heads, part * part_heads, heads, per),
                out_shape=(narrow, narrow, jax.ShapeDtypeStruct((slots, size, size), BF)),
                grid=(1,),
                in_specs=[wide_spec(part)] * 3 + [col_spec, row_spec, init_spec],
                out_specs=(narrow_spec, narrow_spec, state_spec),
                scratch_shapes=scratch,
                compiler_params=pltpu.CompilerParams(
                    collective_id=part,
                    has_side_effects=True,
                    vmem_limit_bytes=63 * 2**20,
                ),
                cost_estimate=estimate(400),
            )(track_query, track_key, track_value, cols, within, initial_state)
        )

    tile = min(16, piece_rows)
    tiles = piece_rows // tile
    lengths = jnp.concatenate([length_of((mine - s) % groups) for s in range(groups)])
    tile_times = (
        time_first + mine * piece_rows + jnp.arange(piece_rows).reshape(tiles, 1, tile)
    )
    key_valid = (tile_times < lengths[None, :, None]).reshape(tiles, all_tracks * tile, 1)
    row_time = jnp.arange(all_tracks * tile) % tile
    same_time = row_time[:, None] == row_time[None, :]
    bias = jnp.where(key_valid & same_time[None], 0.0, -1e30).astype(F32)
    own_block = jnp.reshape(mine * tiles, (1,)).astype(jnp.int32)
    bias_spec = pl.BlockSpec(
        (1, all_tracks * tile, all_tracks * tile), lambda t, own: (t, 0, 0)
    )
    result_spec = pl.BlockSpec((tracks, tile, part_width), lambda t, own: (0, t, 0))
    piece_shape = jax.ShapeDtypeStruct((tracks, piece_rows, part_width), BF)

    back_perms = [[(i, (i - s) % groups) for i in range(groups)] for s in range(groups)]

    def returned(pieces):
        return [
            lax.ppermute(piece, "track", back_perms[s]) if s else piece
            for s, piece in enumerate(pieces)
        ]

    n_all = []
    for part in range(parts):
        normed = forward[part][0]
        n_all.append([normed] + [send(normed, s) for s in range(1, groups)])

    gn_all, gq_all, gk_all = [], [], []
    for part in range(parts):
        own_spec = pl.BlockSpec(
            (tracks, tile, part_width),
            functools.partial(lambda part, t, own: (0, own[0] + t, part), part),
        )
        other_spec = pl.BlockSpec(
            (tracks, tile, part_width), functools.partial(lambda part, t, own: (0, t, part), part)
        )
        own_normed = pl.BlockSpec(
            (tracks, tile, part_width), lambda t, own: (0, own[0] + t, 0)
        )
        cross = pl.pallas_call(
            functools.partial(cross_kernel, groups, part_heads, 1.0 / float(size) ** 0.5),
            out_shape=(piece_shape,) * (3 * groups),
            grid_spec=pltpu.PrefetchScalarGridSpec(
                num_scalar_prefetch=1,
                grid=(tiles,),
                in_specs=[bias_spec]
                + ([own_spec] + [other_spec] * (groups - 1)) * 3
                + [own_normed]
                + [result_spec] * (groups - 1),
                out_specs=(result_spec,) * (3 * groups),
            ),
            compiler_params=pltpu.CompilerParams(vmem_limit_bytes=63 * 2**20),
            cost_estimate=estimate(100),
        )(own_block, bias, *q_parts, *k_parts, *g_parts, *n_all[part])
        gn_all.append(returned(cross[:groups]))
        gq_all.append(returned(cross[groups : 2 * groups]))
        gk_all.append(returned(cross[2 * groups :]))

    def collect(all_pieces, whole_width):
        whole = jnp.zeros((tracks, rows, whole_width), BF)
        for part, pieces in enumerate(all_pieces):
            for s, piece in enumerate(pieces):
                start = ((mine + s) % groups) * piece_rows
                whole = lax.dynamic_update_slice(whole, piece, (0, start, part * part_width))
        return whole

    backward = []
    for part in range(parts):
        grad_normed = collect(gn_all[part : part + 1], part_width)
        backward.append(
            pl.pallas_call(
                functools.partial(
                    backward_kernel, count, part_heads, part * part_heads, heads, per
                ),
                out_shape=(narrow,) * 3,
                grid=(1,),
                in_specs=[wide_spec(part)] * 3
                + [col_spec, row_spec, narrow_spec, narrow_spec, state_spec],
                out_specs=(narrow_spec,) * 3,
                scratch_shapes=scratch,
                compiler_params=pltpu.CompilerParams(
                    collective_id=parts + part,
                    has_side_effects=True,
                    vmem_limit_bytes=63 * 2**20,
                ),
                cost_estimate=estimate(400),
            )(
                track_query,
                track_key,
                track_value,
                cols,
                within,
                forward[part][1],
                grad_normed,
                forward[part][2],
            )
        )

    grads = [
        jnp.concatenate([backward[part][i] for part in range(parts)], axis=2) for i in range(3)
    ]
    return grads[0], grads[1], grads[2], collect(gq_all, width), collect(gk_all, width)


def solution(mesh):
    wide = P("track", "tm", None)
    return jax.shard_map(
        functools.partial(per_device, mesh.shape["tm"], mesh.shape["track"]),
        mesh=mesh,
        in_specs=(
            wide,
            wide,
            wide,
            P("track", None, "tm"),
            P(),
            P("track", None, None, None),
            wide,
            wide,
            wide,
        ),
        out_specs=(wide,) * 5,
        check_vma=False,
    )
```

```python
import functools

import jax
import jax.numpy as jnp
from jax import lax
from jax.experimental import pallas as pl
from jax.experimental.pallas import tpu as pltpu
from jax.sharding import PartitionSpec as P


EPSILON = 1e-06
MESH = pl.DeviceIdType.MESH
BF = jnp.bfloat16
F32 = jnp.float32
HEADS_PER_CHUNK = 1
PARTS = 2


def mm(a, b):
    return lax.dot_general(a, b, (((1,), (0,)), ((), ())), preferred_element_type=F32)


def mm_nt(a, b):
    return lax.dot_general(a, b, (((1,), (1,)), ((), ())), preferred_element_type=F32)


def mm_tn(a, b):
    return lax.dot_general(a, b, (((0,), (0,)), ((), ())), preferred_element_type=F32)


def entry_barrier(me, count):
    barrier = pltpu.get_barrier_semaphore()

    @pl.when(me > 0)
    def _():
        pl.semaphore_signal(barrier, inc=1, device_id={"tm": me - 1}, device_id_type=MESH)

    @pl.when(me < count - 1)
    def _():
        pl.semaphore_signal(barrier, inc=1, device_id={"tm": me + 1}, device_id_type=MESH)

    peers = jnp.where(me > 0, 1, 0) + jnp.where(me < count - 1, 1, 0)
    pl.semaphore_wait(barrier, peers)


def chunk_copy(send_buf, recv_buf, send_sem, recv_sem, chunk, per, target):
    return pltpu.make_async_remote_copy(
        src_ref=send_buf.at[pl.ds(chunk * per, per)],
        dst_ref=recv_buf.at[pl.ds(chunk * per, per)],
        send_sem=send_sem.at[chunk],
        recv_sem=recv_sem.at[chunk],
        device_id={"tm": target},
        device_id_type=MESH,
    )


def split(value):
    high = value.astype(BF)
    return high, (value - high.astype(F32)).astype(BF)


def forward_kernel(
    count, heads, first, lanes, per, q_ref, k_ref, v_ref, col_ref, row_ref, init_ref,
    normed_ref, out_ref, state_ref, recv_buf, send_buf, send_sem, recv_sem,
):
    me = lax.axis_index("tm")
    tracks, rows, width = q_ref.shape
    size = width // heads
    chunks = heads // per
    total = tracks * chunks
    target = jnp.minimum(me + 1, count - 1)
    entry_barrier(me, count)

    @pl.when(me == 0)
    def _():
        def fill(i, carry):
            recv_buf[pl.ds(i * heads, heads)] = init_ref[i].astype(F32)
            return carry

        lax.fori_loop(0, tracks, fill, 0)

    t_index = lax.broadcasted_iota(jnp.int32, (rows, rows), 0)
    s_index = lax.broadcasted_iota(jnp.int32, (rows, rows), 1)
    lower = t_index >= s_index

    def one_track(x, carry):
        cols = col_ref[x]
        valid = cols[:, lanes : lanes + 1]
        from_start = jnp.exp(cols)
        to_end = jnp.exp(cols[rows - 1 : rows, :] - cols)
        for part in range(chunks):
            chunk = x * chunks + part
            sums = []
            keys = []
            for lane in range(per):
                h = part * per + lane
                cut = slice(h * size, (h + 1) * size)
                k_float = k_ref[x, :, cut].astype(F32) * valid
                keys.append(k_float.astype(BF))
                high, low = split(k_float * to_end[:, first + h : first + h + 1])
                v = v_ref[x, :, cut]
                sums.append(mm_tn(high, v) + mm_tn(low, v))

            @pl.when(me > 0)
            def _():
                chunk_copy(send_buf, recv_buf, send_sem, recv_sem, chunk, per, target).wait_recv()

            for lane in range(per):
                h = part * per + lane
                slot = x * heads + h
                send_buf[slot] = (
                    from_start[rows - 1 : rows, first + h : first + h + 1] * recv_buf[slot] + sums[lane]
                )

            @pl.when(me < count - 1)
            def _():
                chunk_copy(send_buf, recv_buf, send_sem, recv_sem, chunk, per, target).start()

            for lane in range(per):
                h = part * per + lane
                slot = x * heads + h
                cut = slice(h * size, (h + 1) * size)
                q = q_ref[x, :, cut]
                state, state_low = split(recv_buf[slot])
                state_ref[slot] = state
                decay = jnp.exp(
                    jnp.where(lower, cols[:, first + h : first + h + 1] - row_ref[x, first + h : first + h + 1, :], -1e30)
                )
                scores, scores_low = split(mm_nt(q, keys[lane]) * decay)
                v = v_ref[x, :, cut]
                late = mm(q, state) + mm(q, state_low)
                outputs = mm(scores, v) + mm(scores_low, v)
                outputs = outputs + from_start[:, first + h : first + h + 1] * late
                square = jnp.mean(outputs * outputs, axis=-1, keepdims=True)
                inverse = lax.rsqrt(square + EPSILON) * valid
                normed_ref[x, :, cut] = (outputs * inverse).astype(BF)
                out_ref[x, :, cut] = outputs.astype(BF)
        return carry

    lax.fori_loop(0, tracks, one_track, 0)

    @pl.when(me < count - 1)
    def _():
        def drain(chunk, carry):
            chunk_copy(send_buf, recv_buf, send_sem, recv_sem, chunk, per, target).wait_send()
            return carry

        lax.fori_loop(0, total, drain, 0)


def backward_kernel(
    count, heads, first, lanes, per, q_ref, k_ref, v_ref, col_ref, row_ref, out_ref, gn_ref, state_ref,
    gq_ref, gk_ref, gv_ref, recv_buf, send_buf, send_sem, recv_sem,
):
    me = lax.axis_index("tm")
    tracks, rows, width = q_ref.shape
    size = width // heads
    chunks = heads // per
    total = tracks * chunks
    target = jnp.maximum(me - 1, 0)
    entry_barrier(me, count)

    @pl.when(me == count - 1)
    def _():
        def fill(i, carry):
            recv_buf[pl.ds(i * heads, heads)] = jnp.zeros((heads, size, size), F32)
            return carry

        lax.fori_loop(0, tracks, fill, 0)

    s_index = lax.broadcasted_iota(jnp.int32, (rows, rows), 0)
    t_index = lax.broadcasted_iota(jnp.int32, (rows, rows), 1)
    upper = t_index >= s_index

    def one_track(x, carry):
        cols = col_ref[x]
        valid = cols[:, lanes : lanes + 1]
        from_start = jnp.exp(cols)
        to_end = jnp.exp(cols[rows - 1 : rows, :] - cols)
        for part in range(chunks):
            chunk = x * chunks + part
            sums = []
            grads = []
            for lane in range(per):
                h = part * per + lane
                cut = slice(h * size, (h + 1) * size)
                outputs = out_ref[x, :, cut].astype(F32)
                square = jnp.mean(outputs * outputs, axis=-1, keepdims=True)
                inverse = lax.rsqrt(square + EPSILON)
                unit = outputs * inverse
                grad = gn_ref[x, :, cut].astype(F32)
                along = jnp.mean(grad * unit, axis=-1, keepdims=True)
                grad = ((inverse * valid) * (grad - unit * along)).astype(BF)
                grads.append(grad)
                q_from = (q_ref[x, :, cut].astype(F32) * from_start[:, first + h : first + h + 1]).astype(BF)
                sums.append(mm_tn(q_from, grad))

            @pl.when(me < count - 1)
            def _():
                chunk_copy(send_buf, recv_buf, send_sem, recv_sem, chunk, per, target).wait_recv()

            for lane in range(per):
                h = part * per + lane
                slot = x * heads + h
                send_buf[slot] = (
                    from_start[rows - 1 : rows, first + h : first + h + 1] * recv_buf[slot] + sums[lane]
                )

            @pl.when(me > 0)
            def _():
                chunk_copy(send_buf, recv_buf, send_sem, recv_sem, chunk, per, target).start()

            for lane in range(per):
                h = part * per + lane
                slot = x * heads + h
                cut = slice(h * size, (h + 1) * size)
                q = q_ref[x, :, cut]
                v = v_ref[x, :, cut]
                key = (k_ref[x, :, cut].astype(F32) * valid).astype(BF)
                grad = grads[lane]
                end_grad = recv_buf[slot].astype(BF)
                decay = jnp.exp(
                    jnp.where(upper, row_ref[x, first + h : first + h + 1, :] - cols[:, first + h : first + h + 1], -1e30)
                )
                grad_scores = (mm_nt(v, grad) * decay).astype(BF)
                scores = (mm_nt(key, q) * decay).astype(BF)
                grad_query = mm_tn(grad_scores, key)
                grad_query = grad_query + from_start[:, first + h : first + h + 1] * mm_nt(grad, state_ref[slot])
                gq_ref[x, :, cut] = grad_query.astype(BF)
                late = to_end[:, first + h : first + h + 1]
                grad_key = mm(grad_scores, q) + late * mm_nt(v, end_grad)
                gk_ref[x, :, cut] = (grad_key * valid).astype(BF)
                grad_value = mm(scores, grad) + late * mm(key, end_grad)
                gv_ref[x, :, cut] = grad_value.astype(BF)
        return carry

    lax.fori_loop(0, tracks, one_track, 0)

    @pl.when(me > 0)
    def _():
        def drain(chunk, carry):
            chunk_copy(send_buf, recv_buf, send_sem, recv_sem, chunk, per, target).wait_send()
            return carry

        lax.fori_loop(0, total, drain, 0)


def cross_kernel(groups, heads, scale, own_ref, bias_ref, *refs):
    q_refs, k_refs, g_refs, n_refs = (refs[i * groups : (i + 1) * groups] for i in range(4))
    outs = refs[4 * groups :]
    gn_outs, gq_outs, gk_outs = (outs[i * groups : (i + 1) * groups] for i in range(3))
    tracks, rows, width = q_refs[0].shape
    size = width // heads
    piece = tracks * rows

    def load(parts, cut):
        return jnp.concatenate([part[:, :, cut].reshape(piece, size) for part in parts], axis=0)

    def store(parts, cut, value):
        for i, part in enumerate(parts):
            part[:, :, cut] = value[i * piece : (i + 1) * piece].astype(BF).reshape(
                tracks, rows, size
            )

    bias = bias_ref[0]
    for h in range(heads):
        cut = slice(h * size, (h + 1) * size)
        q, k, g, n = (load(parts, cut) for parts in (q_refs, k_refs, g_refs, n_refs))
        logits = mm_nt(k, q) * scale + bias
        top = jnp.max(logits, axis=0, keepdims=True)
        weights = jnp.exp(logits - top)
        weights = weights * (1.0 / jnp.sum(weights, axis=0, keepdims=True))
        grad_weights = mm_nt(n, g)
        weighted = weights * grad_weights
        grad_logits = (weighted - weights * jnp.sum(weighted, axis=0, keepdims=True)) * scale
        grad_logits = grad_logits.astype(BF)
        store(gn_outs, cut, mm(weights.astype(BF), g))
        store(gq_outs, cut, mm_tn(grad_logits, k))
        store(gk_outs, cut, mm(grad_logits, q))


def per_device(
    count,
    groups,
    track_query,
    track_key,
    track_value,
    log_decay,
    valid_length,
    initial_state,
    cross_query,
    cross_key,
    grad_out,
):
    tracks, rows, width = track_query.shape
    heads = log_decay.shape[1]
    size = width // heads
    parts = PARTS if heads % PARTS == 0 else 1
    part_heads = heads // parts
    part_width = width // parts
    per = HEADS_PER_CHUNK if part_heads % HEADS_PER_CHUNK == 0 else 1
    chunks = part_heads // per
    slots = tracks * part_heads
    all_tracks = valid_length.shape[0]
    mine = lax.axis_index("track")
    time_first = lax.axis_index("tm") * rows
    piece_rows = rows // groups

    grouped = valid_length.reshape(groups, tracks)
    length_of = lambda group: lax.dynamic_index_in_dim(grouped, group, 0, keepdims=False)
    own_length = length_of(mine)
    times = time_first + jnp.arange(rows)
    valid = (times[None, :] < own_length[:, None]).astype(F32)

    triangle = (jnp.arange(rows)[:, None] <= jnp.arange(rows)[None, :]).astype(F32)
    within = jnp.einsum("xhs,st->xht", log_decay, triangle, precision=lax.Precision.HIGHEST)
    cols = jnp.concatenate(
        [
            jnp.transpose(within, (0, 2, 1)),
            valid[:, :, None],
            jnp.zeros((tracks, rows, 128 - heads - 1), F32),
        ],
        axis=2,
    )

    def send(value, shift):
        perm = [(i, (i + shift) % groups) for i in range(groups)]
        start = ((mine + shift) % groups) * piece_rows
        piece = lax.dynamic_slice_in_dim(value, start, piece_rows, axis=1)
        return lax.ppermute(piece, "track", perm)

    grad_masked = grad_out * valid[:, :, None].astype(BF)
    q_parts = [cross_query] + [send(cross_query, s) for s in range(1, groups)]
    k_parts = [cross_key] + [send(cross_key, s) for s in range(1, groups)]
    g_parts = [grad_masked] + [send(grad_masked, s) for s in range(1, groups)]

    once = pl.Buffered(1)

    def wide_spec(part):
        return pl.BlockSpec(
            (tracks, rows, part_width), lambda i: (0, 0, part), pipeline_mode=once
        )

    narrow_spec = wide_spec(0)
    col_spec = pl.BlockSpec((tracks, rows, 128), lambda i: (0, 0, 0), pipeline_mode=once)
    row_spec = pl.BlockSpec((tracks, heads, rows), lambda i: (0, 0, 0), pipeline_mode=once)
    state_spec = pl.BlockSpec((slots, size, size), lambda i: (0, 0, 0), pipeline_mode=once)
    narrow = jax.ShapeDtypeStruct((tracks, rows, part_width), BF)
    scratch = [
        pltpu.VMEM((slots, size, size), F32),
        pltpu.VMEM((slots, size, size), F32),
        pltpu.SemaphoreType.DMA((tracks * chunks,)),
        pltpu.SemaphoreType.DMA((tracks * chunks,)),
    ]
    dot_flops = 2 * slots * rows * size * size

    def estimate(times_over):
        return pl.CostEstimate(
            flops=times_over * dot_flops,
            bytes_accessed=16 * slots * size * size,
            transcendentals=0,
        )

    forward = []
    for part in range(parts):
        init_spec = pl.BlockSpec(
            (tracks, part_heads, size, size),
            functools.partial(lambda part, i: (0, part, 0, 0), part),
            pipeline_mode=once,
        )
        forward.append(
            pl.pallas_call(
                functools.partial(forward_kernel, count, part_heads, part * part_heads, heads, per),
                out_shape=(narrow, narrow, jax.ShapeDtypeStruct((slots, size, size), BF)),
                grid=(1,),
                in_specs=[wide_spec(part)] * 3 + [col_spec, row_spec, init_spec],
                out_specs=(narrow_spec, narrow_spec, state_spec),
                scratch_shapes=scratch,
                compiler_params=pltpu.CompilerParams(
                    collective_id=part,
                    has_side_effects=True,
                    vmem_limit_bytes=28 * 2**20,
                ),
                cost_estimate=estimate(400),
            )(track_query, track_key, track_value, cols, within, initial_state)
        )

    tile = min(16, piece_rows)
    tiles = piece_rows // tile
    lengths = jnp.concatenate([length_of((mine - s) % groups) for s in range(groups)])
    tile_times = (
        time_first + mine * piece_rows + jnp.arange(piece_rows).reshape(tiles, 1, tile)
    )
    key_valid = (tile_times < lengths[None, :, None]).reshape(tiles, all_tracks * tile, 1)
    row_time = jnp.arange(all_tracks * tile) % tile
    same_time = row_time[:, None] == row_time[None, :]
    bias = jnp.where(key_valid & same_time[None], 0.0, -1e30).astype(F32)
    own_block = jnp.reshape(mine * tiles, (1,)).astype(jnp.int32)
    bias_spec = pl.BlockSpec(
        (1, all_tracks * tile, all_tracks * tile), lambda t, own: (t, 0, 0)
    )
    result_spec = pl.BlockSpec((tracks, tile, part_width), lambda t, own: (0, t, 0))
    piece_shape = jax.ShapeDtypeStruct((tracks, piece_rows, part_width), BF)

    back_perms = [[(i, (i - s) % groups) for i in range(groups)] for s in range(groups)]

    def returned(pieces):
        return [
            lax.ppermute(piece, "track", back_perms[s]) if s else piece
            for s, piece in enumerate(pieces)
        ]

    n_all = []
    for part in range(parts):
        normed = forward[part][0]
        n_all.append([normed] + [send(normed, s) for s in range(1, groups)])

    gn_all, gq_all, gk_all = [], [], []
    for part in range(parts):
        own_spec = pl.BlockSpec(
            (tracks, tile, part_width),
            functools.partial(lambda part, t, own: (0, own[0] + t, part), part),
        )
        other_spec = pl.BlockSpec(
            (tracks, tile, part_width), functools.partial(lambda part, t, own: (0, t, part), part)
        )
        own_normed = pl.BlockSpec(
            (tracks, tile, part_width), lambda t, own: (0, own[0] + t, 0)
        )
        cross = pl.pallas_call(
            functools.partial(cross_kernel, groups, part_heads, 1.0 / float(size) ** 0.5),
            out_shape=(piece_shape,) * (3 * groups),
            grid_spec=pltpu.PrefetchScalarGridSpec(
                num_scalar_prefetch=1,
                grid=(tiles,),
                in_specs=[bias_spec]
                + ([own_spec] + [other_spec] * (groups - 1)) * 3
                + [own_normed]
                + [result_spec] * (groups - 1),
                out_specs=(result_spec,) * (3 * groups),
            ),
            compiler_params=pltpu.CompilerParams(vmem_limit_bytes=28 * 2**20),
            cost_estimate=estimate(100),
        )(own_block, bias, *q_parts, *k_parts, *g_parts, *n_all[part])
        gn_all.append(returned(cross[:groups]))
        gq_all.append(returned(cross[groups : 2 * groups]))
        gk_all.append(returned(cross[2 * groups :]))

    def collect(all_pieces, whole_width):
        whole = jnp.zeros((tracks, rows, whole_width), BF)
        for part, pieces in enumerate(all_pieces):
            for s, piece in enumerate(pieces):
                start = ((mine + s) % groups) * piece_rows
                whole = lax.dynamic_update_slice(whole, piece, (0, start, part * part_width))
        return whole

    backward = []
    for part in range(parts):
        grad_normed = collect(gn_all[part : part + 1], part_width)
        backward.append(
            pl.pallas_call(
                functools.partial(
                    backward_kernel, count, part_heads, part * part_heads, heads, per
                ),
                out_shape=(narrow,) * 3,
                grid=(1,),
                in_specs=[wide_spec(part)] * 3
                + [col_spec, row_spec, narrow_spec, narrow_spec, state_spec],
                out_specs=(narrow_spec,) * 3,
                scratch_shapes=scratch,
                compiler_params=pltpu.CompilerParams(
                    collective_id=parts + part,
                    has_side_effects=True,
                    vmem_limit_bytes=28 * 2**20,
                ),
                cost_estimate=estimate(400),
            )(
                track_query,
                track_key,
                track_value,
                cols,
                within,
                forward[part][1],
                grad_normed,
                forward[part][2],
            )
        )

    grads = [
        jnp.concatenate([backward[part][i] for part in range(parts)], axis=2) for i in range(3)
    ]
    return grads[0], grads[1], grads[2], collect(gq_all, width), collect(gk_all, width)


def solution(mesh):
    wide = P("track", "tm", None)
    return jax.shard_map(
        functools.partial(per_device, mesh.shape["tm"], mesh.shape["track"]),
        mesh=mesh,
        in_specs=(
            wide,
            wide,
            wide,
            P("track", None, "tm"),
            P(),
            P("track", None, None, None),
            wide,
            wide,
            wide,
        ),
        out_specs=(wide,) * 5,
        check_vma=False,
    )
```
